32 devices in a mesh: obs: 8 (over z, core), spec: 4 (over y, x).
Axes of the slice: x: 2, y: 2, z: 4, core: 2. Of those that a mesh axis runs over, the one named last changes fastest.
Arguments:
- departures: bfloat16 [448, 131072], P(None, ('obs', 'spec')), may hold values from -6 to 6
- stencil_cols: int32 [1024, 128, 4], P('obs'), may hold values from 0 to 127
- stencil_wts: bfloat16 [1024, 128, 4], P('obs'), may hold values from 0.049804688 to 1
- dest_dev: int32 [1024, 1], P('obs'), may hold values from 0 to 7; in each aligned block of 128 rows (0 to 127, 128 to 255, ...) at most 32 rows name the same one
- dest_block: int32 [1024], P('obs'), may hold values from 0 to 79
- block_counts: int32 [8], P('obs'), may hold values from 1 to 128, 768 in all
Outputs:
- fourier: bfloat16 [2560, 448, 32], P('obs', 'spec')
The draws below stay inside these ranges and needn't reach their ends.
Inputs may be any that keep to these rules, and one draw needn't show every extreme that they name: `dest_dev`: among the 128 blocks of one index of obs at most 32 name one owner; some index reaches it. `block_counts`: blocks of an index from its count on are padding and their departures are ignored; some index has all 128 valid.
All inputs are finite; a program needn't handle non-finite values.
Results may differ from the reference program's by a relative error of at most 0.0055.
Values may be sent and summed in bfloat16 or wider, within the bound.
A program may use at most 128 MiB of HBM per device.

```python
import math
import jax
import jax.numpy as jnp
import numpy as np
from jax import lax

NLON = 2560
STENCIL = 4
NB_DEV = 128
CH = 448
CAP = 32
NBLK = 1024
NOBS = 131072
GB_DEV = 80
NLAT = 32
N_OBS = 8


def with_ends(result, stream_key, smallest, top_value):
    place = [jax.random.randint(jax.random.fold_in(stream_key, axis), (), 0, length) for axis, length in enumerate(result.shape)]
    main_axis = result.shape.index(max(result.shape))
    neighbour = place[:main_axis] + [(place[main_axis] + 1) % result.shape[main_axis]] + place[main_axis + 1:]
    return result.at[tuple(place)].set(smallest).at[tuple(neighbour)].set(top_value)


def block_levels(own_key, dims, pieces, smallest, top_value):
    level = 1.0
    for position, shards_of in pieces:
        heights = jax.random.uniform(jax.random.fold_in(jax.random.fold_in(own_key, 6), position), (shards_of,), jnp.float32, smallest / len(pieces), top_value / len(pieces))
        level = level * jnp.repeat(jnp.exp(heights), dims[position] // shards_of).reshape((-1,) + (1,) * (len(dims) - 1 - position))
    return level


def profile(amount, total, bound, lean):
    portions = [(1 << 20) // math.isqrt(standing ** lean) + 1 for standing in range(2, amount + 1)]
    spare, holding = total - bound - (amount - 1), [1] * (amount - 1)
    while spare > 0:
        free = [i for i in range(amount - 1) if holding[i] < bound]
        mass, budget = sum([portions[i] for i in free]), spare
        for i in free:
            extra = min(bound - holding[i], max(1, budget * portions[i] // mass), spare)
            holding[i] = holding[i] + extra
            spare = spare - extra
    return np.array([bound] + holding)


def uneven(rng, number_of, total, limit, lean):
    if number_of == 2:
        one = jax.random.randint(rng, (), max(1, total - limit), min(limit, total - 1) + 1)
        return jnp.stack([one, total - one])
    tallies = jnp.asarray(profile(number_of, total, limit, lean), jnp.int32)
    twos = (number_of - 1) // 2
    source_of, taker = tallies[1:1 + 2 * twos:2], tallies[2:2 + 2 * twos:2]
    room = jnp.minimum(source_of - 1, limit - taker)
    shifted = jax.random.randint(jax.random.fold_in(rng, 1), (twos,), 0, 1 << 20) % (room + 1)
    tallies = tallies.at[1:1 + 2 * twos:2].set(source_of - shifted).at[2:2 + 2 * twos:2].set(taker + shifted)
    return tallies[jax.random.permutation(jax.random.fold_in(rng, 2), number_of)]


def shared_out(key, own, number, rows, number_of, top, most, lean):
    order = jax.random.permutation(key, number_of)
    packed, ordinary = shares(number_of, rows * top, most, lean, True), shares(number_of, rows * top, most, lean, False)
    places = jnp.arange(number_of)

    def named(sizes, rotation):
        used = int((sizes > 0).sum())
        fixed = max(1, used // 4)
        shifted = fixed + (places - fixed + rotation * (used - fixed)) % max(1, number_of - fixed)
        return jnp.zeros((number_of,), jnp.int32).at[order[jnp.where(places < fixed, places, shifted)]].set(jnp.asarray(sizes, jnp.int32))

    sizes = jnp.where(number % 4 == 0, named(packed, number // 4), named(ordinary, number - number // 4 - 1))
    mixed = jax.random.permutation(jax.random.fold_in(own, 3), number_of)
    source_of, sink = mixed[0:number_of // 2 * 2:2], mixed[1:number_of // 2 * 2:2]
    margin = jnp.minimum(sizes[source_of] - 1, most - sizes[sink]) // 2
    margin = jnp.where((source_of == order[0]) | (sink == order[0]) | (sizes[sink] == 0), 0, jnp.maximum(margin, 0))
    shifted = jax.random.randint(jax.random.fold_in(own, 4), (number_of // 2,), 0, 1 << 20) % (margin + 1)
    sizes = sizes.at[source_of].add(-shifted).at[sink].add(shifted)
    members = jnp.searchsorted(jnp.cumsum(sizes), jnp.arange(rows * top), side="right").astype(jnp.int32)
    table = members.reshape(top, rows).T
    table = table[jax.random.permutation(jax.random.fold_in(own, 1), rows)]
    rotation = jax.random.randint(jax.random.fold_in(own, 2), (rows, 1), 0, top)
    return jnp.take_along_axis(table, (jnp.arange(top)[None, :] + rotation) % top, axis=1)


def shares(number_of, total, reach, slope, full):
    portions = [(1 << 20) // math.isqrt(grade ** slope) + 1 for grade in range(1, number_of + 1)]
    largest = reach if full else min(reach, max(-(-total // number_of), total * portions[0] // sum(portions)))
    least = 1 if total - largest >= number_of - 1 else 0
    counts, spare = [largest] + [least] * (number_of - 1), total - largest - least * (number_of - 1)
    while spare > 0:
        free = [i for i in range(1, number_of) if counts[i] < largest] or [i for i in range(1, number_of) if counts[i] < reach]
        whole, budget = sum([portions[i] for i in free]), spare
        for i in free:
            extra = min(reach - counts[i], max(1, budget * portions[i] // whole), spare)
            counts[i] = counts[i] + extra
            spare = spare - extra
    return np.array(counts)


def bell_draw(rng, extent, scale, reach, split=(), kind=jnp.bfloat16):
    array = scale * jax.random.normal(rng, extent, jnp.float32)
    if split:
        array = array * block_levels(rng, extent, split, -0.22, 0.18)
    return jnp.clip(array, -reach, reach).astype(kind)


def setup_inputs(seed: int = 0) -> dict:
    key_of = jax.random.split(jax.random.key(seed), 7)
    departures = bell_draw(key_of[0], (CH, NOBS), 1.0, 6.0, ((1, 32),))
    stencil_cols = with_ends(jax.random.randint(key_of[1], (NBLK, 128, STENCIL), 0, 128), jax.random.fold_in(key_of[1], 1), 0, 127).astype(jnp.int32)
    stencil_wts = jnp.clip(0.049804688 + 0.9501953 * jax.random.uniform(key_of[2], (NBLK, 128, STENCIL), jnp.float32) ** block_levels(key_of[2], (NBLK, 128, STENCIL), ((0, 8),), -0.2, 0.2), 0.049804688, 1.0).astype(jnp.bfloat16)
    dest_dev_keys = jax.random.split(jax.random.fold_in(key_of[3], 1), NBLK // NB_DEV)
    dest_dev_turns = jax.random.permutation(jax.random.fold_in(key_of[3], 3), NBLK // NB_DEV)
    dest_dev = jax.vmap(lambda own, number: shared_out(jax.random.fold_in(key_of[3], 2), own, number, NB_DEV, N_OBS, 1, CAP, 2))(dest_dev_keys, dest_dev_turns).reshape((NBLK, 1))
    dest_block = with_ends(jax.random.randint(key_of[4], (NBLK,), 0, GB_DEV), jax.random.fold_in(key_of[4], 1), 0, GB_DEV - 1).astype(jnp.int32)
    block_counts = uneven(key_of[5], N_OBS, N_OBS * NB_DEV * 3 // 4, NB_DEV, 2).astype(jnp.int32)
    return {"departures": departures, "stencil_cols": stencil_cols, "stencil_wts": stencil_wts, "dest_dev": dest_dev, "dest_block": dest_block, "block_counts": block_counts}


def stencil_matrix(columns, weights):
    targets = jnp.arange(128, dtype=jnp.int32)
    matches = (columns[..., None] == targets).astype(jnp.float32)
    return jnp.sum(weights.astype(jnp.float32)[..., None] * matches, axis=-2)


def fourier_table(longitudes, first, modes):
    wavenumbers = first + jnp.arange(modes, dtype=jnp.int32)
    points = jnp.arange(longitudes, dtype=jnp.int32)
    phase = (points[:, None] * wavenumbers[None, :]) % longitudes
    angles = phase.astype(jnp.float32) * (2.0 * jnp.pi / longitudes)
    factor = jnp.where(wavenumbers == 0, 1.0, 2.0).astype(jnp.float32)
    cosines = factor[None, :] * jnp.cos(angles)
    sines = -factor[None, :] * jnp.sin(angles)
    return jnp.stack([cosines, sines], axis=2).reshape(longitudes, 2 * modes)


def reference(departures, stencil_cols, stencil_wts, dest_dev, dest_block, block_counts):
    channels = departures.shape[0]
    grouped = departures.reshape(channels, N_OBS, NB_DEV, 128)

    def step(grid, group):
        start = (group * NB_DEV).astype(jnp.int32)
        span_dep = lax.dynamic_index_in_dim(grouped, group, 1, keepdims=False)
        valid = (jnp.arange(NB_DEV, dtype=jnp.int32) < block_counts[group]).astype(jnp.bfloat16)
        masked = span_dep * valid[None, :, None]
        columns = lax.dynamic_slice_in_dim(stencil_cols, start, NB_DEV, 0)
        weights = lax.dynamic_slice_in_dim(stencil_wts, start, NB_DEV, 0)
        owners = lax.dynamic_slice_in_dim(dest_dev[:, 0], start, NB_DEV, 0)
        blocks = lax.dynamic_slice_in_dim(dest_block, start, NB_DEV, 0)
        stencil = stencil_matrix(columns, weights)
        contribution = jnp.einsum('cbo,bog->cbg', masked.astype(jnp.float32), stencil, precision=lax.Precision.HIGHEST)
        targets = (owners * GB_DEV + blocks).astype(jnp.int32)
        return grid.at[:, targets].add(contribution), None

    start_grid = jnp.zeros((channels, GB_DEV * N_OBS, 128), jnp.float32)
    grid, unused = lax.scan(step, start_grid, jnp.arange(N_OBS, dtype=jnp.int32))
    grid_bf = grid.reshape(channels, NLAT, NLON).astype(jnp.bfloat16)
    table = fourier_table(NLON, 0, NLON // 2).astype(jnp.bfloat16)
    fourier = jnp.einsum('clj,jk->kcl', grid_bf.astype(jnp.float32), table.astype(jnp.float32))
    return fourier.astype(jnp.bfloat16)
```

```python
import jax
import jax.numpy as jnp
from jax import lax
from jax.sharding import PartitionSpec as P

NLON = 2560
LAT_DEV = 4


def contribute(dep_blocks, columns, weights, form):
    targets = jnp.arange(128, dtype=jnp.int32)
    total = None
    for point in range(columns.shape[2]):
        matches = (columns[:, :, point, None] == targets).astype(jnp.bfloat16)
        single = weights[:, :, point, None] * matches
        term = jnp.einsum(form, dep_blocks, single, preferred_element_type=jnp.float32)
        total = term if total is None else total + term
    return total


def fourier_table(longitudes, first, modes):
    wavenumbers = first + jnp.arange(modes, dtype=jnp.int32)
    points = jnp.arange(longitudes, dtype=jnp.int32)
    phase = points[:, None] * wavenumbers[None, :] % longitudes
    angles = phase.astype(jnp.float32) * (2.0 * jnp.pi / longitudes)
    factor = jnp.where(wavenumbers == 0, 1.0, 2.0).astype(jnp.float32)
    cosines = factor[None, :] * jnp.cos(angles)
    sines = -factor[None, :] * jnp.sin(angles)
    return jnp.stack([cosines, sines], axis=2).reshape(longitudes, 2 * modes)


def shards(departures, stencil_cols, stencil_wts, dest_dev, dest_block, block_counts):
    owners_count = lax.axis_size("obs")
    local_dep = lax.all_to_all(departures, "spec", split_axis=0, concat_axis=1, tiled=True)
    channels = local_dep.shape[0]
    blocks = stencil_cols.shape[0]
    capacity = max(2, 2 * blocks // owners_count)
    valid = (jnp.arange(blocks, dtype=jnp.int32) < block_counts[0]).astype(jnp.bfloat16)
    masked = local_dep.reshape(channels, blocks, 128) * valid[None, :, None]
    target = dest_dev[:, 0]
    matches = (target[:, None] == jnp.arange(owners_count, dtype=jnp.int32)[None, :]).astype(
        jnp.int32
    )
    ranking = jnp.sum(jnp.cumsum(matches, axis=0) * matches, axis=1) - 1
    slot_of = target * capacity + ranking
    slots = owners_count * capacity
    labels = jnp.full((slots,), -1, jnp.int32).at[slot_of].set(dest_block)
    partial_sums = contribute(masked, stencil_cols, stencil_wts, "cbo,bog->bcg")
    outgoing = jnp.zeros((slots, channels, 128), jnp.float32).at[slot_of].set(partial_sums)
    incoming, got_labels = (
        lax.all_to_all(outgoing, "obs", split_axis=0, concat_axis=0, tiled=True),
        lax.all_to_all(labels, "obs", split_axis=0, concat_axis=0, tiled=True),
    )
    grid_blocks = LAT_DEV * NLON // 128
    places = jnp.where(got_labels < 0, grid_blocks, got_labels)
    summed = jnp.zeros((grid_blocks + 1, channels, 128), jnp.float32).at[places].add(incoming)
    grid = jnp.transpose(summed[:grid_blocks], (1, 0, 2))
    grid_bf = grid.reshape(channels, LAT_DEV, NLON).astype(jnp.bfloat16)

    def analyse(block_index):
        table = fourier_table(NLON, block_index * 128, 128).astype(jnp.bfloat16)
        return jnp.einsum("clj,jk->kcl", grid_bf, table, preferred_element_type=jnp.float32).astype(
            jnp.bfloat16
        )

    coefficients = lax.map(analyse, jnp.arange(NLON // 256, dtype=jnp.int32))
    coefficients = coefficients.reshape(NLON, channels, LAT_DEV)
    return lax.all_to_all(coefficients, "obs", split_axis=0, concat_axis=2, tiled=True)


CHUNKS = (32, 48, 32)


def turned_table(first, modes):
    index = first + jnp.arange(modes, dtype=jnp.int32)
    wavenumbers, odd = index // 2, index % 2 == 1

    def turns(points):
        phase = points[:, None] * wavenumbers[None, :] % NLON
        angles = phase.astype(jnp.float32) * (2.0 * jnp.pi / NLON)
        return jnp.cos(angles), jnp.sin(angles)

    cos_block, sin_block = turns(128 * jnp.arange(NLON // 128, dtype=jnp.int32))
    cos_point, sin_point = turns(jnp.arange(128, dtype=jnp.int32))
    factor = jnp.where(wavenumbers == 0, 1.0, 2.0).astype(jnp.float32)
    first_part = factor * jnp.where(odd, -sin_block, cos_block)
    second_part = factor * jnp.where(odd, cos_block, sin_block)
    product = first_part[:, None] * cos_point[None] - second_part[:, None] * sin_point[None]
    return product.astype(jnp.bfloat16)


def line_shards(departures, stencil_cols, stencil_wts, dest_dev, dest_block, block_counts):
    obs = lax.axis_index("obs")
    specs = lax.axis_size("spec")
    core, chip = obs % 2, obs // 2
    right = chip // 2
    inner = (chip == 1) | (chip == 2)
    blocks = stencil_cols.shape[0]
    part = blocks // specs
    channels = departures.shape[0] // specs
    grid_blocks = 8 * LAT_DEV * NLON // 128
    half = NLON // 2
    swap = [(i, i ^ 1) for i in range(8)]
    inward = [(0, 2), (1, 3), (6, 4), (7, 5)]
    middle = [(2, 4), (3, 5), (4, 2), (5, 3)]
    outward = [(2, 0), (3, 1), (4, 6), (5, 7)]

    split = departures.reshape(specs, channels, departures.shape[1])
    starts = [sum(CHUNKS[:i]) for i in range(len(CHUNKS))]
    received = [
        lax.all_to_all(split[:, s : s + n], "spec", split_axis=0, concat_axis=0, tiled=True)
        for s, n in zip(starts, CHUNKS)
    ]

    lanes = jnp.arange(128, dtype=jnp.int32)
    valid = jnp.arange(blocks, dtype=jnp.int32) < block_counts[0]
    weights = jnp.where(valid[:, None, None], stencil_wts, 0).astype(jnp.float32)
    stencil = None
    for point in range(stencil_cols.shape[2]):
        term = jnp.where(stencil_cols[:, :, point, None] == lanes, weights[:, :, point, None], 0.0)
        stencil = term if stencil is None else stencil + term
    stencil = stencil.astype(jnp.bfloat16).reshape(specs, part, 128, 128)

    target = dest_dev[:, 0] * (grid_blocks // 8) + dest_block
    every = lax.all_gather(target, "obs", axis=0, tiled=False)
    mates = jnp.stack([obs, obs ^ 1, 6 * right + core, 6 * right + (core ^ 1)])
    targets = jnp.take(every, mates, axis=0).reshape(-1)
    onehot = (jnp.arange(grid_blocks, dtype=jnp.int32)[:, None] == targets[None, :]).astype(jnp.bfloat16)

    table_own = turned_table(right * half, half)
    table_other = turned_table((1 - right) * half, half)

    results = []
    for dep, count in zip(received, CHUNKS):
        own = count // 2
        dep = dep.reshape(specs, count, part, 128)
        pieces = jnp.einsum("pcbo,pboj->pbcj", dep, stencil, preferred_element_type=jnp.float32)
        pieces = pieces.astype(jnp.bfloat16).reshape(blocks, 2, own, 128)
        kept = lax.dynamic_index_in_dim(pieces, core, 1, keepdims=False)
        given = lax.dynamic_index_in_dim(pieces, 1 - core, 1, keepdims=False)
        far_kept = lax.ppermute(kept, "obs", inward)
        taken = lax.ppermute(given, "obs", swap)
        far_taken = lax.ppermute(taken, "obs", inward)
        slots = jnp.concatenate([kept, taken, far_kept, far_taken], axis=0)
        grid = jnp.einsum("qs,scj->qcj", onehot, slots, preferred_element_type=jnp.float32)
        grid = grid.astype(jnp.bfloat16).reshape(-1, NLON // 128, own, 128)
        sent = jnp.einsum("lbcj,bjk->klc", grid, table_other, preferred_element_type=jnp.float32)
        sent = sent.astype(jnp.bfloat16).reshape(half, -1)
        crossed = lax.ppermute(sent, "obs", middle)
        stay = jnp.einsum("lbcj,bjk->klc", grid, table_own, preferred_element_type=jnp.float32)
        total = (stay.reshape(half, -1) + crossed.astype(jnp.float32)).astype(jnp.bfloat16)
        quarter = half // 2
        nearer = lax.dynamic_slice_in_dim(total, (1 - right) * quarter, quarter, 0)
        farther = lax.dynamic_slice_in_dim(total, right * quarter, quarter, 0)
        handed = lax.ppermute(farther, "obs", outward)
        mine = jnp.where(inner, nearer, handed)
        eighth = quarter // 2
        lower = lax.dynamic_slice_in_dim(mine, core * eighth, eighth, 0)
        other = lax.dynamic_slice_in_dim(mine, (1 - core) * eighth, eighth, 0)
        back = lax.ppermute(other, "obs", swap)
        lower, back = (a.reshape(eighth, -1, own) for a in (lower, back))
        results.append(jnp.where(core == 0, lower, back))
        results.append(jnp.where(core == 0, back, lower))
    return jnp.transpose(jnp.concatenate(results, axis=2), (0, 2, 1))


def solution(mesh):
    in_specs = (
        P(None, ("obs", "spec")),
        P("obs", None, None),
        P("obs", None, None),
        P("obs", None),
        P("obs"),
        P("obs"),
    )
    out_specs = P("obs", "spec", None)
    body = line_shards if mesh.shape["obs"] == 8 and mesh.shape["spec"] == 4 else shards
    return jax.shard_map(body, mesh=mesh, in_specs=in_specs, out_specs=out_specs, check_vma=False)
```

```python
import jax
import jax.numpy as jnp
from jax import lax
from jax.experimental import pallas as pl
from jax.experimental.pallas import tpu as pltpu
from jax.sharding import PartitionSpec as P

NLON = 2560
LAT_DEV = 4


def contribute(dep_blocks, columns, weights, form):
    targets = jnp.arange(128, dtype=jnp.int32)
    total = None
    for point in range(columns.shape[2]):
        matches = (columns[:, :, point, None] == targets).astype(jnp.bfloat16)
        single = weights[:, :, point, None] * matches
        term = jnp.einsum(form, dep_blocks, single, preferred_element_type=jnp.float32)
        total = term if total is None else total + term
    return total


def fourier_table(longitudes, first, modes):
    wavenumbers = first + jnp.arange(modes, dtype=jnp.int32)
    points = jnp.arange(longitudes, dtype=jnp.int32)
    phase = points[:, None] * wavenumbers[None, :] % longitudes
    angles = phase.astype(jnp.float32) * (2.0 * jnp.pi / longitudes)
    factor = jnp.where(wavenumbers == 0, 1.0, 2.0).astype(jnp.float32)
    cosines = factor[None, :] * jnp.cos(angles)
    sines = -factor[None, :] * jnp.sin(angles)
    return jnp.stack([cosines, sines], axis=2).reshape(longitudes, 2 * modes)


def shards(departures, stencil_cols, stencil_wts, dest_dev, dest_block, block_counts):
    owners_count = lax.axis_size("obs")
    local_dep = lax.all_to_all(departures, "spec", split_axis=0, concat_axis=1, tiled=True)
    channels = local_dep.shape[0]
    blocks = stencil_cols.shape[0]
    capacity = max(2, 2 * blocks // owners_count)
    valid = (jnp.arange(blocks, dtype=jnp.int32) < block_counts[0]).astype(jnp.bfloat16)
    masked = local_dep.reshape(channels, blocks, 128) * valid[None, :, None]
    target = dest_dev[:, 0]
    matches = (target[:, None] == jnp.arange(owners_count, dtype=jnp.int32)[None, :]).astype(
        jnp.int32
    )
    ranking = jnp.sum(jnp.cumsum(matches, axis=0) * matches, axis=1) - 1
    slot_of = target * capacity + ranking
    slots = owners_count * capacity
    labels = jnp.full((slots,), -1, jnp.int32).at[slot_of].set(dest_block)
    partial_sums = contribute(masked, stencil_cols, stencil_wts, "cbo,bog->bcg")
    outgoing = jnp.zeros((slots, channels, 128), jnp.float32).at[slot_of].set(partial_sums)
    incoming, got_labels = (
        lax.all_to_all(outgoing, "obs", split_axis=0, concat_axis=0, tiled=True),
        lax.all_to_all(labels, "obs", split_axis=0, concat_axis=0, tiled=True),
    )
    grid_blocks = LAT_DEV * NLON // 128
    places = jnp.where(got_labels < 0, grid_blocks, got_labels)
    summed = jnp.zeros((grid_blocks + 1, channels, 128), jnp.float32).at[places].add(incoming)
    grid = jnp.transpose(summed[:grid_blocks], (1, 0, 2))
    grid_bf = grid.reshape(channels, LAT_DEV, NLON).astype(jnp.bfloat16)

    def analyse(block_index):
        table = fourier_table(NLON, block_index * 128, 128).astype(jnp.bfloat16)
        return jnp.einsum("clj,jk->kcl", grid_bf, table, preferred_element_type=jnp.float32).astype(
            jnp.bfloat16
        )

    coefficients = lax.map(analyse, jnp.arange(NLON // 256, dtype=jnp.int32))
    coefficients = coefficients.reshape(NLON, channels, LAT_DEV)
    return lax.all_to_all(coefficients, "obs", split_axis=0, concat_axis=2, tiled=True)


CHUNKS = (32, 48, 32)


def turned_table(first, modes):
    index = first + jnp.arange(modes, dtype=jnp.int32)
    wavenumbers, odd = index // 2, index % 2 == 1

    def turns(points):
        phase = points[:, None] * wavenumbers[None, :] % NLON
        angles = phase.astype(jnp.float32) * (2.0 * jnp.pi / NLON)
        return jnp.cos(angles), jnp.sin(angles)

    cos_block, sin_block = turns(128 * jnp.arange(NLON // 128, dtype=jnp.int32))
    cos_point, sin_point = turns(jnp.arange(128, dtype=jnp.int32))
    factor = jnp.where(wavenumbers == 0, 1.0, 2.0).astype(jnp.float32)
    first_part = factor * jnp.where(odd, -sin_block, cos_block)
    second_part = factor * jnp.where(odd, cos_block, sin_block)
    product = first_part[:, None] * cos_point[None] - second_part[:, None] * sin_point[None]
    return product.astype(jnp.bfloat16)


GROUP = 16


def pieces_kernel(core_ref, dep_ref, stencil_ref, kept_ref, given_ref):
    own = kept_ref.shape[0]
    pieces = [
        lax.dot_general(
            dep_ref[0, :, 128 * b : 128 * (b + 1)],
            stencil_ref[b],
            (((1,), (1,)), ((), ())),
            preferred_element_type=jnp.float32,
        )
        for b in range(GROUP)
    ]
    pieces = jnp.stack(pieces, axis=1)
    low, high = pieces[:own], pieces[own:]
    first = core_ref[0] == 0
    kept_ref[...] = jnp.where(first, low, high).astype(jnp.bfloat16)
    given_ref[...] = jnp.where(first, high, low).astype(jnp.bfloat16)


def contributions(core, dep, stencil):
    specs, channels, _ = dep.shape
    blocks = stencil.shape[0]
    groups = blocks // GROUP
    per_spec = groups // specs
    own = channels // 2
    out = jax.ShapeDtypeStruct((own, blocks, 128), jnp.bfloat16)
    out_spec = pl.BlockSpec((own, GROUP, 128), lambda g, core_ref: (0, g, 0))
    return pl.pallas_call(
        pieces_kernel,
        out_shape=(out, out),
        grid_spec=pltpu.PrefetchScalarGridSpec(
            num_scalar_prefetch=1,
            grid=(groups,),
            in_specs=[
                pl.BlockSpec((1, channels, GROUP * 128), lambda g, core_ref: (g // per_spec, 0, g % per_spec)),
                pl.BlockSpec((GROUP, 128, 128), lambda g, core_ref: (g, 0, 0)),
            ],
            out_specs=(out_spec, out_spec),
        ),
        cost_estimate=pl.CostEstimate(
            flops=2 * blocks * 128 * 128 * channels, bytes_accessed=3 * blocks * 128 * 128, transcendentals=0
        ),
        name="contributions",
    )(core, dep, stencil)


def line_shards(departures, stencil_cols, stencil_wts, dest_dev, dest_block, block_counts):
    obs = lax.axis_index("obs")
    specs = lax.axis_size("spec")
    core, chip = obs % 2, obs // 2
    right = chip // 2
    inner = (chip == 1) | (chip == 2)
    blocks = stencil_cols.shape[0]
    part = blocks // specs
    channels = departures.shape[0] // specs
    grid_blocks = 8 * LAT_DEV * NLON // 128
    half = NLON // 2
    swap = [(i, i ^ 1) for i in range(8)]
    inward = [(0, 2), (1, 3), (6, 4), (7, 5)]
    middle = [(2, 4), (3, 5), (4, 2), (5, 3)]
    outward = [(2, 0), (3, 1), (4, 6), (5, 7)]

    split = departures.reshape(specs, channels, departures.shape[1])
    starts = [sum(CHUNKS[:i]) for i in range(len(CHUNKS))]
    received = [
        lax.all_to_all(split[:, s : s + n], "spec", split_axis=0, concat_axis=0, tiled=True)
        for s, n in zip(starts, CHUNKS)
    ]

    points = jnp.arange(128, dtype=jnp.int32)[:, None]
    valid = jnp.arange(blocks, dtype=jnp.int32) < block_counts[0]
    weights = jnp.where(valid[:, None, None], stencil_wts, 0).astype(jnp.float32)
    columns, weights = jnp.swapaxes(stencil_cols, 1, 2), jnp.swapaxes(weights, 1, 2)
    stencil = None
    for point in range(columns.shape[1]):
        term = jnp.where(columns[:, point, None, :] == points, weights[:, point, None, :], 0.0)
        stencil = term if stencil is None else stencil + term
    stencil = stencil.astype(jnp.bfloat16)

    near = dest_dev[:, 0] * (grid_blocks // 8) + dest_block
    mate = lax.ppermute(near, "obs", swap)
    near = jnp.concatenate([near, mate])
    targets = jnp.concatenate([near, lax.ppermute(near, "obs", inward)])
    onehot = (jnp.arange(grid_blocks, dtype=jnp.int32)[:, None] == targets[None, :]).astype(jnp.bfloat16)

    table_own = turned_table(right * half, half)
    table_other = turned_table((1 - right) * half, half)

    results = []
    core_operand = core[None].astype(jnp.int32)
    for dep, count in zip(received, CHUNKS):
        own = count // 2
        kept, given = contributions(core_operand, dep, stencil)
        far_kept = lax.ppermute(kept, "obs", inward)
        taken = lax.ppermute(given, "obs", swap)
        far_taken = lax.ppermute(taken, "obs", inward)
        slots = jnp.concatenate([kept, taken, far_kept, far_taken], axis=1)
        grid = jnp.einsum("qs,csj->cqj", onehot, slots, preferred_element_type=jnp.float32)
        grid = grid.astype(jnp.bfloat16).reshape(own, -1, NLON // 128, 128)
        sent = jnp.einsum("clbj,bjk->lck", grid, table_other, preferred_element_type=jnp.float32)
        crossed = lax.ppermute(sent.astype(jnp.bfloat16), "obs", middle)
        stay = jnp.einsum("clbj,bjk->lck", grid, table_own, preferred_element_type=jnp.float32)
        total = (stay + crossed.astype(jnp.float32)).astype(jnp.bfloat16)
        quarter = half // 2
        nearer = lax.dynamic_slice_in_dim(total, (1 - right) * quarter, quarter, 2)
        farther = lax.dynamic_slice_in_dim(total, right * quarter, quarter, 2)
        handed = lax.ppermute(farther, "obs", outward)
        mine = jnp.where(inner, nearer, handed)
        eighth = quarter // 2
        first, second = mine[:, :, :eighth], mine[:, :, eighth:]
        lower = jnp.where(core == 0, first, second)
        back = lax.ppermute(jnp.where(core == 0, second, first), "obs", swap)
        results.append(jnp.where(core == 0, lower, back))
        results.append(jnp.where(core == 0, back, lower))
    return jnp.transpose(jnp.concatenate(results, axis=1), (2, 1, 0))


def solution(mesh):
    in_specs = (
        P(None, ("obs", "spec")),
        P("obs", None, None),
        P("obs", None, None),
        P("obs", None),
        P("obs"),
        P("obs"),
    )
    out_specs = P("obs", "spec", None)
    body = line_shards if mesh.shape["obs"] == 8 and mesh.shape["spec"] == 4 else shards
    return jax.shard_map(body, mesh=mesh, in_specs=in_specs, out_specs=out_specs, check_vma=False)
```

```python
import jax
import jax.numpy as jnp
from jax import lax
from jax.experimental import pallas as pl
from jax.experimental.pallas import tpu as pltpu
from jax.sharding import PartitionSpec as P

NLON = 2560
LAT_DEV = 4


def contribute(dep_blocks, columns, weights, form):
    targets = jnp.arange(128, dtype=jnp.int32)
    total = None
    for point in range(columns.shape[2]):
        matches = (columns[:, :, point, None] == targets).astype(jnp.bfloat16)
        single = weights[:, :, point, None] * matches
        term = jnp.einsum(form, dep_blocks, single, preferred_element_type=jnp.float32)
        total = term if total is None else total + term
    return total


def fourier_table(longitudes, first, modes):
    wavenumbers = first + jnp.arange(modes, dtype=jnp.int32)
    points = jnp.arange(longitudes, dtype=jnp.int32)
    phase = points[:, None] * wavenumbers[None, :] % longitudes
    angles = phase.astype(jnp.float32) * (2.0 * jnp.pi / longitudes)
    factor = jnp.where(wavenumbers == 0, 1.0, 2.0).astype(jnp.float32)
    cosines = factor[None, :] * jnp.cos(angles)
    sines = -factor[None, :] * jnp.sin(angles)
    return jnp.stack([cosines, sines], axis=2).reshape(longitudes, 2 * modes)


def shards(departures, stencil_cols, stencil_wts, dest_dev, dest_block, block_counts):
    owners_count = lax.axis_size("obs")
    local_dep = lax.all_to_all(departures, "spec", split_axis=0, concat_axis=1, tiled=True)
    channels = local_dep.shape[0]
    blocks = stencil_cols.shape[0]
    capacity = max(2, 2 * blocks // owners_count)
    valid = (jnp.arange(blocks, dtype=jnp.int32) < block_counts[0]).astype(jnp.bfloat16)
    masked = local_dep.reshape(channels, blocks, 128) * valid[None, :, None]
    target = dest_dev[:, 0]
    matches = (target[:, None] == jnp.arange(owners_count, dtype=jnp.int32)[None, :]).astype(
        jnp.int32
    )
    ranking = jnp.sum(jnp.cumsum(matches, axis=0) * matches, axis=1) - 1
    slot_of = target * capacity + ranking
    slots = owners_count * capacity
    labels = jnp.full((slots,), -1, jnp.int32).at[slot_of].set(dest_block)
    partial_sums = contribute(masked, stencil_cols, stencil_wts, "cbo,bog->bcg")
    outgoing = jnp.zeros((slots, channels, 128), jnp.float32).at[slot_of].set(partial_sums)
    incoming, got_labels = (
        lax.all_to_all(outgoing, "obs", split_axis=0, concat_axis=0, tiled=True),
        lax.all_to_all(labels, "obs", split_axis=0, concat_axis=0, tiled=True),
    )
    grid_blocks = LAT_DEV * NLON // 128
    places = jnp.where(got_labels < 0, grid_blocks, got_labels)
    summed = jnp.zeros((grid_blocks + 1, channels, 128), jnp.float32).at[places].add(incoming)
    grid = jnp.transpose(summed[:grid_blocks], (1, 0, 2))
    grid_bf = grid.reshape(channels, LAT_DEV, NLON).astype(jnp.bfloat16)

    def analyse(block_index):
        table = fourier_table(NLON, block_index * 128, 128).astype(jnp.bfloat16)
        return jnp.einsum("clj,jk->kcl", grid_bf, table, preferred_element_type=jnp.float32).astype(
            jnp.bfloat16
        )

    coefficients = lax.map(analyse, jnp.arange(NLON // 256, dtype=jnp.int32))
    coefficients = coefficients.reshape(NLON, channels, LAT_DEV)
    return lax.all_to_all(coefficients, "obs", split_axis=0, concat_axis=2, tiled=True)


CHUNKS = (32, 48, 32)


def turned_table(first, modes):
    index = first + jnp.arange(modes, dtype=jnp.int32)
    wavenumbers, odd = index // 2, index % 2 == 1

    def turns(points):
        phase = points[:, None] * wavenumbers[None, :] % NLON
        angles = phase.astype(jnp.float32) * (2.0 * jnp.pi / NLON)
        return jnp.cos(angles), jnp.sin(angles)

    cos_block, sin_block = turns(128 * jnp.arange(NLON // 128, dtype=jnp.int32))
    cos_point, sin_point = turns(jnp.arange(128, dtype=jnp.int32))
    factor = jnp.where(wavenumbers == 0, 1.0, 2.0).astype(jnp.float32)
    first_part = factor * jnp.where(odd, -sin_block, cos_block)
    second_part = factor * jnp.where(odd, cos_block, sin_block)
    product = first_part[:, None] * cos_point[None] - second_part[:, None] * sin_point[None]
    return product.astype(jnp.bfloat16)


GROUP = 16


def pieces_kernel(core_ref, dep_ref, stencil_ref, kept_ref, given_ref):
    own = kept_ref.shape[0]
    pieces = [
        lax.dot_general(
            dep_ref[0, :, 128 * b : 128 * (b + 1)],
            stencil_ref[b],
            (((1,), (1,)), ((), ())),
            preferred_element_type=jnp.float32,
        )
        for b in range(GROUP)
    ]
    pieces = jnp.stack(pieces, axis=1)
    low, high = pieces[:own], pieces[own:]
    first = core_ref[0] == 0
    kept_ref[...] = jnp.where(first, low, high).astype(jnp.bfloat16)
    given_ref[...] = jnp.where(first, high, low).astype(jnp.bfloat16)


def contributions(core, dep, stencil):
    specs, channels, _ = dep.shape
    blocks = stencil.shape[0]
    groups = blocks // GROUP
    per_spec = groups // specs
    own = channels // 2
    out = jax.ShapeDtypeStruct((own, blocks, 128), jnp.bfloat16)
    out_spec = pl.BlockSpec((own, GROUP, 128), lambda g, core_ref: (0, g, 0))
    return pl.pallas_call(
        pieces_kernel,
        out_shape=(out, out),
        grid_spec=pltpu.PrefetchScalarGridSpec(
            num_scalar_prefetch=1,
            grid=(groups,),
            in_specs=[
                pl.BlockSpec((1, channels, GROUP * 128), lambda g, core_ref: (g // per_spec, 0, g % per_spec)),
                pl.BlockSpec((GROUP, 128, 128), lambda g, core_ref: (g, 0, 0)),
            ],
            out_specs=(out_spec, out_spec),
        ),
        cost_estimate=pl.CostEstimate(
            flops=2 * blocks * 128 * 128 * channels, bytes_accessed=3 * blocks * 128 * 128, transcendentals=0
        ),
        name="contributions",
    )(core, dep, stencil)


def line_shards(departures, stencil_cols, stencil_wts, dest_dev, dest_block, block_counts):
    obs = lax.axis_index("obs")
    specs = lax.axis_size("spec")
    core, chip = obs % 2, obs // 2
    right = chip // 2
    inner = (chip == 1) | (chip == 2)
    blocks = stencil_cols.shape[0]
    part = blocks // specs
    channels = departures.shape[0] // specs
    grid_blocks = 8 * LAT_DEV * NLON // 128
    half = NLON // 2
    swap = [(i, i ^ 1) for i in range(8)]
    inward = [(0, 2), (1, 3), (6, 4), (7, 5)]
    middle = [(2, 4), (3, 5), (4, 2), (5, 3)]
    outward = [(2, 0), (3, 1), (4, 6), (5, 7)]
    inward_across = [(0, 3), (1, 2), (6, 5), (7, 4)]
    outward_across = [(2, 1), (3, 0), (4, 7), (5, 6)]
    swap_inner = [(2, 3), (3, 2), (4, 5), (5, 4)]

    split = departures.reshape(specs, channels, departures.shape[1])
    starts = [sum(CHUNKS[:i]) for i in range(len(CHUNKS))]
    points = jnp.arange(128, dtype=jnp.int32)[:, None]
    valid = jnp.arange(blocks, dtype=jnp.int32) < block_counts[0]
    weights = jnp.where(valid[:, None, None], stencil_wts, 0).astype(jnp.float32)
    columns, weights = jnp.swapaxes(stencil_cols, 1, 2), jnp.swapaxes(weights, 1, 2)
    stencil = None
    for point in range(columns.shape[1]):
        term = jnp.where(columns[:, point, None, :] == points, weights[:, point, None, :], 0.0)
        stencil = term if stencil is None else stencil + term
    stencil = stencil.astype(jnp.bfloat16)

    near = dest_dev[:, 0] * (grid_blocks // 8) + dest_block
    pairs = (swap, inward, inward_across)
    targets = jnp.concatenate([near] + [lax.ppermute(near, "obs", pair) for pair in pairs])
    onehot = (jnp.arange(grid_blocks, dtype=jnp.int32)[:, None] == targets[None, :]).astype(jnp.bfloat16)

    table_own = turned_table(right * half, half)
    table_other = turned_table((1 - right) * half, half)

    results = []
    core_operand = core[None].astype(jnp.int32)
    inputs = [split[:, s : s + n] for s, n in zip(starts, CHUNKS)]
    inputs[1], stencil, onehot, table_own, table_other = lax.optimization_barrier(
        (inputs[1], stencil, onehot, table_own, table_other)
    )
    received = {}

    def receive(number):
        received[number] = lax.all_to_all(inputs[number], "spec", split_axis=0, concat_axis=0, tiled=True)

    receive(0)
    receive(1)
    eighth = half // 4

    def place(pieces, index):
        return jnp.where(index < 2, jnp.where(index == 0, pieces[0], pieces[1]), jnp.where(index == 2, pieces[2], pieces[3]))

    crossings, sums = [], []
    for number, count in enumerate(CHUNKS):
        own = count // 2
        dep = received[number]
        if number >= 2:
            dep, sums[number - 2] = lax.optimization_barrier((dep, sums[number - 2]))
            crossings.append(lax.ppermute(sums[number - 2], "obs", middle))
        kept, given = contributions(core_operand, dep, stencil)
        if number + 2 < len(CHUNKS):
            inputs[number + 2], kept, given = lax.optimization_barrier((inputs[number + 2], kept, given))
            receive(number + 2)
        far_kept = lax.ppermute(kept, "obs", inward)
        far_taken = lax.ppermute(given, "obs", inward_across)
        taken = lax.ppermute(given, "obs", swap)
        if number >= 2:
            far_taken, crossings[number - 2] = lax.optimization_barrier((far_taken, crossings[number - 2]))
        slots = jnp.concatenate([kept, taken, far_kept, far_taken], axis=1)
        grid = jnp.einsum("qs,csj->cqj", onehot, slots, preferred_element_type=jnp.float32)
        grid = grid.astype(jnp.bfloat16).reshape(own, -1, NLON // 128, 128)
        sent = jnp.einsum("clbj,bjk->lck", grid, table_other, preferred_element_type=jnp.float32)
        sums.append(sent.astype(jnp.bfloat16))
        results.append(grid)
    crossings += [lax.ppermute(each, "obs", middle) for each in sums[-2:]]
    grids, results = results, []
    for grid, crossed in zip(grids, crossings):
        stay = jnp.einsum("clbj,bjk->lck", grid, table_own, preferred_element_type=jnp.float32)
        total = (stay + crossed.astype(jnp.float32)).astype(jnp.bfloat16)
        pieces = [total[:, :, eighth * i : eighth * (i + 1)] for i in range(4)]
        outer, near = 2 * right, 2 - 2 * right
        handed = lax.ppermute(place(pieces, outer + core), "obs", outward)
        handed_across = lax.ppermute(place(pieces, outer + (1 - core)), "obs", outward_across)
        back = lax.ppermute(place(pieces, near + (1 - core)), "obs", swap_inner)
        mine = jnp.where(inner, place(pieces, near + core), handed)
        other = jnp.where(inner, back, handed_across)
        results.append(jnp.where(core == 0, mine, other))
        results.append(jnp.where(core == 0, other, mine))
    return jnp.transpose(jnp.concatenate(results, axis=1), (2, 1, 0))


def solution(mesh):
    in_specs = (
        P(None, ("obs", "spec")),
        P("obs", None, None),
        P("obs", None, None),
        P("obs", None),
        P("obs"),
        P("obs"),
    )
    out_specs = P("obs", "spec", None)
    body = line_shards if mesh.shape["obs"] == 8 and mesh.shape["spec"] == 4 else shards
    return jax.shard_map(body, mesh=mesh, in_specs=in_specs, out_specs=out_specs, check_vma=False)
```

```python
import jax
import jax.numpy as jnp
from jax import lax
from jax.experimental import pallas as pl
from jax.experimental.pallas import tpu as pltpu
from jax.sharding import PartitionSpec as P

NLON = 2560
LAT_DEV = 4


def contribute(dep_blocks, columns, weights, form):
    targets = jnp.arange(128, dtype=jnp.int32)
    total = None
    for point in range(columns.shape[2]):
        matches = (columns[:, :, point, None] == targets).astype(jnp.bfloat16)
        single = weights[:, :, point, None] * matches
        term = jnp.einsum(form, dep_blocks, single, preferred_element_type=jnp.float32)
        total = term if total is None else total + term
    return total


def fourier_table(longitudes, first, modes):
    wavenumbers = first + jnp.arange(modes, dtype=jnp.int32)
    points = jnp.arange(longitudes, dtype=jnp.int32)
    phase = points[:, None] * wavenumbers[None, :] % longitudes
    angles = phase.astype(jnp.float32) * (2.0 * jnp.pi / longitudes)
    factor = jnp.where(wavenumbers == 0, 1.0, 2.0).astype(jnp.float32)
    cosines = factor[None, :] * jnp.cos(angles)
    sines = -factor[None, :] * jnp.sin(angles)
    return jnp.stack([cosines, sines], axis=2).reshape(longitudes, 2 * modes)


def shards(departures, stencil_cols, stencil_wts, dest_dev, dest_block, block_counts):
    owners_count = lax.axis_size("obs")
    local_dep = lax.all_to_all(departures, "spec", split_axis=0, concat_axis=1, tiled=True)
    channels = local_dep.shape[0]
    blocks = stencil_cols.shape[0]
    capacity = max(2, 2 * blocks // owners_count)
    valid = (jnp.arange(blocks, dtype=jnp.int32) < block_counts[0]).astype(jnp.bfloat16)
    masked = local_dep.reshape(channels, blocks, 128) * valid[None, :, None]
    target = dest_dev[:, 0]
    matches = (target[:, None] == jnp.arange(owners_count, dtype=jnp.int32)[None, :]).astype(
        jnp.int32
    )
    ranking = jnp.sum(jnp.cumsum(matches, axis=0) * matches, axis=1) - 1
    slot_of = target * capacity + ranking
    slots = owners_count * capacity
    labels = jnp.full((slots,), -1, jnp.int32).at[slot_of].set(dest_block)
    partial_sums = contribute(masked, stencil_cols, stencil_wts, "cbo,bog->bcg")
    outgoing = jnp.zeros((slots, channels, 128), jnp.float32).at[slot_of].set(partial_sums)
    incoming, got_labels = (
        lax.all_to_all(outgoing, "obs", split_axis=0, concat_axis=0, tiled=True),
        lax.all_to_all(labels, "obs", split_axis=0, concat_axis=0, tiled=True),
    )
    grid_blocks = LAT_DEV * NLON // 128
    places = jnp.where(got_labels < 0, grid_blocks, got_labels)
    summed = jnp.zeros((grid_blocks + 1, channels, 128), jnp.float32).at[places].add(incoming)
    grid = jnp.transpose(summed[:grid_blocks], (1, 0, 2))
    grid_bf = grid.reshape(channels, LAT_DEV, NLON).astype(jnp.bfloat16)

    def analyse(block_index):
        table = fourier_table(NLON, block_index * 128, 128).astype(jnp.bfloat16)
        return jnp.einsum("clj,jk->kcl", grid_bf, table, preferred_element_type=jnp.float32).astype(
            jnp.bfloat16
        )

    coefficients = lax.map(analyse, jnp.arange(NLON // 256, dtype=jnp.int32))
    coefficients = coefficients.reshape(NLON, channels, LAT_DEV)
    return lax.all_to_all(coefficients, "obs", split_axis=0, concat_axis=2, tiled=True)


CHUNKS = (32, 48, 32)


def turned_table(first, modes):
    index = first + jnp.arange(modes, dtype=jnp.int32)
    wavenumbers, odd = index // 2, index % 2 == 1

    def turns(points):
        phase = points[:, None] * wavenumbers[None, :] % NLON
        angles = phase.astype(jnp.float32) * (2.0 * jnp.pi / NLON)
        return jnp.cos(angles), jnp.sin(angles)

    cos_block, sin_block = turns(128 * jnp.arange(NLON // 128, dtype=jnp.int32))
    cos_point, sin_point = turns(jnp.arange(128, dtype=jnp.int32))
    factor = jnp.where(wavenumbers == 0, 1.0, 2.0).astype(jnp.float32)
    first_part = factor * jnp.where(odd, -sin_block, cos_block)
    second_part = factor * jnp.where(odd, cos_block, sin_block)
    product = first_part[:, None] * cos_point[None] - second_part[:, None] * sin_point[None]
    return product.astype(jnp.bfloat16)


GROUP = 16


def pieces_kernel(core_ref, dep_ref, stencil_ref, kept_ref, given_ref):
    own = kept_ref.shape[0]
    pieces = [
        lax.dot_general(
            dep_ref[0, :, 128 * b : 128 * (b + 1)],
            stencil_ref[b],
            (((1,), (1,)), ((), ())),
            preferred_element_type=jnp.float32,
        )
        for b in range(GROUP)
    ]
    pieces = jnp.stack(pieces, axis=1)
    low, high = pieces[:own], pieces[own:]
    first = core_ref[0] == 0
    kept_ref[...] = jnp.where(first, low, high).astype(jnp.bfloat16)
    given_ref[...] = jnp.where(first, high, low).astype(jnp.bfloat16)


def contributions(core, dep, stencil):
    specs, channels, _ = dep.shape
    blocks = stencil.shape[0]
    groups = blocks // GROUP
    per_spec = groups // specs
    own = channels // 2
    out = jax.ShapeDtypeStruct((own, blocks, 128), jnp.bfloat16)
    out_spec = pl.BlockSpec((own, GROUP, 128), lambda g, core_ref: (0, g, 0))
    return pl.pallas_call(
        pieces_kernel,
        out_shape=(out, out),
        grid_spec=pltpu.PrefetchScalarGridSpec(
            num_scalar_prefetch=1,
            grid=(groups,),
            in_specs=[
                pl.BlockSpec((1, channels, GROUP * 128), lambda g, core_ref: (g // per_spec, 0, g % per_spec)),
                pl.BlockSpec((GROUP, 128, 128), lambda g, core_ref: (g, 0, 0)),
            ],
            out_specs=(out_spec, out_spec),
        ),
        cost_estimate=pl.CostEstimate(
            flops=2 * blocks * 128 * 128 * channels, bytes_accessed=3 * blocks * 128 * 128, transcendentals=0
        ),
        name="contributions",
    )(core, dep, stencil)


def line_shards(departures, stencil_cols, stencil_wts, dest_dev, dest_block, block_counts):
    obs = lax.axis_index("obs")
    specs = lax.axis_size("spec")
    core, chip = obs % 2, obs // 2
    right = chip // 2
    inner = (chip == 1) | (chip == 2)
    blocks = stencil_cols.shape[0]
    part = blocks // specs
    channels = departures.shape[0] // specs
    grid_blocks = 8 * LAT_DEV * NLON // 128
    half = NLON // 2
    swap = [(i, i ^ 1) for i in range(8)]
    inward = [(0, 2), (1, 3), (6, 4), (7, 5)]
    middle = [(2, 4), (3, 5), (4, 2), (5, 3)]
    outward = [(2, 0), (3, 1), (4, 6), (5, 7)]
    inward_across = [(0, 3), (1, 2), (6, 5), (7, 4)]
    outward_across = [(2, 1), (3, 0), (4, 7), (5, 6)]
    swap_inner = [(2, 3), (3, 2), (4, 5), (5, 4)]

    split = departures.reshape(specs, channels, departures.shape[1])
    starts = [sum(CHUNKS[:i]) for i in range(len(CHUNKS))]
    points = jnp.arange(128, dtype=jnp.int32)[:, None]
    valid = jnp.arange(blocks, dtype=jnp.int32) < block_counts[0]
    weights = jnp.where(valid[:, None, None], stencil_wts, 0).astype(jnp.float32)
    columns, weights = jnp.swapaxes(stencil_cols, 1, 2), jnp.swapaxes(weights, 1, 2)
    stencil = None
    for point in range(columns.shape[1]):
        term = jnp.where(columns[:, point, None, :] == points, weights[:, point, None, :], 0.0)
        stencil = term if stencil is None else stencil + term
    stencil = stencil.astype(jnp.bfloat16)

    near = dest_dev[:, 0] * (grid_blocks // 8) + dest_block
    pairs = (swap, inward, inward_across)
    targets = jnp.concatenate([near] + [lax.ppermute(near, "obs", pair) for pair in pairs])
    onehot = (jnp.arange(grid_blocks, dtype=jnp.int32)[:, None] == targets[None, :]).astype(jnp.bfloat16)

    table_own = turned_table(right * half, half)
    table_other = turned_table((1 - right) * half, half)

    results = []
    core_operand = core[None].astype(jnp.int32)
    inputs = [split[:, s : s + n] for s, n in zip(starts, CHUNKS)]
    inputs[1], stencil, onehot, table_own, table_other = lax.optimization_barrier(
        (inputs[1], stencil, onehot, table_own, table_other)
    )
    received = {}

    def receive(number):
        received[number] = lax.all_to_all(inputs[number], "spec", split_axis=0, concat_axis=0, tiled=True)

    receive(0)
    receive(1)
    eighth = half // 4

    def place(pieces, index):
        return jnp.where(index < 2, jnp.where(index == 0, pieces[0], pieces[1]), jnp.where(index == 2, pieces[2], pieces[3]))

    crossings, sums = [], []
    for number, count in enumerate(CHUNKS):
        own = count // 2
        dep = received[number]
        if number >= 2:
            dep, sums[number - 2] = lax.optimization_barrier((dep, sums[number - 2]))
            crossings.append(lax.ppermute(sums[number - 2], "obs", middle))
        kept, given = contributions(core_operand, dep, stencil)
        if number + 2 < len(CHUNKS):
            inputs[number + 2], kept, given = lax.optimization_barrier((inputs[number + 2], kept, given))
            receive(number + 2)
        far_kept = lax.ppermute(kept, "obs", inward)
        far_taken = lax.ppermute(given, "obs", inward_across)
        taken = lax.ppermute(given, "obs", swap)
        if number >= 2:
            far_taken, crossings[number - 2] = lax.optimization_barrier((far_taken, crossings[number - 2]))
        slots = jnp.concatenate([kept, taken, far_kept, far_taken], axis=1)
        slots = jnp.swapaxes(slots, 0, 1)
        grid = jnp.einsum("qs,scj->qcj", onehot, slots, preferred_element_type=jnp.float32)
        grid = grid.astype(jnp.bfloat16).reshape(-1, NLON // 128, own, 128)
        sent = jnp.einsum("lbcj,bjk->lck", grid, table_other, preferred_element_type=jnp.float32)
        sums.append(sent.astype(jnp.bfloat16))
        results.append(grid)
    crossings += [lax.ppermute(each, "obs", middle) for each in sums[-2:]]
    grids, results = results, []
    for grid, crossed in zip(grids, crossings):
        stay = jnp.einsum("lbcj,bjk->lck", grid, table_own, preferred_element_type=jnp.float32)
        total = (stay + crossed.astype(jnp.float32)).astype(jnp.bfloat16)
        pieces = [total[:, :, eighth * i : eighth * (i + 1)] for i in range(4)]
        outer, near = 2 * right, 2 - 2 * right
        handed = lax.ppermute(place(pieces, outer + core), "obs", outward)
        handed_across = lax.ppermute(place(pieces, outer + (1 - core)), "obs", outward_across)
        back = lax.ppermute(place(pieces, near + (1 - core)), "obs", swap_inner)
        mine = jnp.where(inner, place(pieces, near + core), handed)
        other = jnp.where(inner, back, handed_across)
        results.append(jnp.where(core == 0, mine, other))
        results.append(jnp.where(core == 0, other, mine))
    return jnp.transpose(jnp.concatenate(results, axis=1), (2, 1, 0))


def solution(mesh):
    in_specs = (
        P(None, ("obs", "spec")),
        P("obs", None, None),
        P("obs", None, None),
        P("obs", None),
        P("obs"),
        P("obs"),
    )
    out_specs = P("obs", "spec", None)
    body = line_shards if mesh.shape["obs"] == 8 and mesh.shape["spec"] == 4 else shards
    return jax.shard_map(body, mesh=mesh, in_specs=in_specs, out_specs=out_specs, check_vma=False)
```
